768 devices in a mesh: mem: 4 (over x), reg: 192 (over z, y, core).
Axes of the slice: x: 4, y: 8, z: 12, core: 2. Of those that a mesh axis runs over, the one named last changes fastest.
Arguments:
- members: bfloat16 [512, 6144, 128], P('mem', 'reg'), may hold values from -6 to 6
- diffusivity: float32 [6144, 128], P('reg'), may hold values from 0.02 to 0.2
- advection: float32 [6144, 128], P('reg'), may hold values from -0.3 to 0.3
- obs_value: bfloat16 [192, 4, 256], P('reg', 'mem'), may hold values from -6 to 6
- obs_rinv: float32 [192, 4, 256], P('reg', 'mem'), may hold values from 0.5 to 4
- obs_cell: int32 [192, 4, 256], P('reg', 'mem'), may hold values from 0 to 1023
- obs_count: int32 [192, 4], P('reg', 'mem'), may hold values from 64 to 256, as said below
- loc_index: int32 [192, 4, 256], P('reg', 'mem'), may hold values from 0 to 7
Outputs:
- analysis: float32 [512, 6144, 128], P('mem', 'reg')
The draws below stay inside these ranges and needn't reach their ends.
Inputs may be any that keep to these rules, and one draw needn't show every extreme that they name: `obs_count`: each patch has 64 to 256 live slots, and some patch has exactly 256.
All inputs are finite; a program needn't handle non-finite values.
Results may differ from the reference program's by a relative error of at most 0.0047.
Values may be sent and summed in bfloat16 or wider, within the bound.
No kernel may reach another device: no remote copies, remote signals or barrier semaphores. Data moves between devices by JAX's collectives and lax.ppermute only.
A program may use at most 32 MiB of HBM per device.

```python
import math
import jax
import jax.numpy as jnp
from jax import lax

ENSEMBLE_SIZE = 512
TILE_LINES = 8
LATTICE_BREADTH = 128
OWN = 256
STEPS = 3
NSIT = 2
ZONE_TOTAL = 192
GRID_ROWS = 6144
N_MEM = 4


def draw_obs_count(key, part):
    first_key, second_key = jax.random.split(jax.random.fold_in(key, 7))
    counts = jax.random.randint(first_key, (ZONE_TOTAL * N_MEM,), OWN // 4, OWN + 1, dtype=jnp.int32)
    chosen = jax.random.randint(second_key, (), 0, ZONE_TOTAL * N_MEM, dtype=jnp.int32)
    counts = jnp.where(jnp.arange(ZONE_TOTAL * N_MEM, dtype=jnp.int32) == chosen, OWN, counts)
    return counts.reshape(ZONE_TOTAL, N_MEM)


def plant(array, own_key, smallest, high):
    longest = array.shape.index(max(array.shape))
    spots = []
    for shift in (0, 1):
        where = [jax.random.randint(jax.random.fold_in(own_key, axis), (), 0, length) for axis, length in enumerate(array.shape)]
        where[longest] = (where[longest] + shift) % array.shape[longest]
        spots.append(tuple(where))
    return array.at[spots[0]].set(smallest).at[spots[1]].set(high)


def steps_of(key, shape, shards, low, top_value):
    level = 1.0
    for axis_at, parts in shards:
        heights = jax.random.uniform(jax.random.fold_in(jax.random.fold_in(key, 6), axis_at), (parts,), jnp.float32, low / len(shards), top_value / len(shards))
        level = level * jnp.repeat(jnp.exp(heights), shape[axis_at] // parts).reshape((-1,) + (1,) * (len(shape) - 1 - axis_at))
    return level


def noise(own_key, dims, scale, most, pieces=(), held_as=jnp.bfloat16):
    loudness = steps_of(own_key, dims, pieces, -0.22, 0.18) if pieces else 1.0
    values = jax.random.normal(own_key, dims, jnp.float32) * scale * loudness
    return jnp.minimum(jnp.maximum(values, -most), most).astype(held_as)


def setup_inputs(seed: int = 0) -> dict:
    key_of = jax.random.split(jax.random.key(seed), 9)
    return {
        "members": noise(key_of[0], (ENSEMBLE_SIZE, GRID_ROWS, LATTICE_BREADTH), 1.0, 6.0, ((0, 4), (1, 192))),
        "diffusivity": jnp.clip(jnp.exp(math.log(0.2) - 2.3025851 * jax.random.uniform(key_of[1], (GRID_ROWS, LATTICE_BREADTH), jnp.float32) ** steps_of(key_of[1], (GRID_ROWS, LATTICE_BREADTH), ((0, 192),), -0.2, 0.2)), 0.02, 0.2),
        "advection": jnp.clip(jax.random.uniform(key_of[2], (GRID_ROWS, LATTICE_BREADTH), jnp.float32, -0.3, 0.3) * steps_of(key_of[2], (GRID_ROWS, LATTICE_BREADTH), ((0, 192),), -0.4, 0.0), -0.3, 0.3),
        "obs_value": noise(key_of[3], (ZONE_TOTAL, N_MEM, OWN), 1.0, 6.0, ((0, 192), (1, 4))),
        "obs_rinv": jnp.clip(jnp.exp(math.log(4.0) - 2.0794415 * jax.random.uniform(key_of[4], (ZONE_TOTAL, N_MEM, OWN), jnp.float32) ** steps_of(key_of[4], (ZONE_TOTAL, N_MEM, OWN), ((0, 192), (1, 4)), -0.2, 0.2)), 0.5, 4.0),
        "obs_cell": plant(jax.random.randint(key_of[5], (ZONE_TOTAL, N_MEM, OWN), 0, TILE_LINES * LATTICE_BREADTH), jax.random.fold_in(key_of[5], 1), 0, (TILE_LINES * LATTICE_BREADTH) - 1).astype(jnp.int32),
        "obs_count": draw_obs_count(jax.random.fold_in(key_of[8], 71), 0),
        "loc_index": plant(jax.random.randint(key_of[7], (ZONE_TOTAL, N_MEM, OWN), 0, 8), jax.random.fold_in(key_of[7], 1), 0, 7).astype(jnp.int32),
    }


def advance_all(ensemble_sample_array, diffusivity, advection):
    north_row = jnp.roll(ensemble_sample_array, 1, 1)
    south_row = jnp.roll(ensemble_sample_array, -1, 1)
    east_cell = jnp.roll(ensemble_sample_array, -1, 2)
    west_cell = jnp.roll(ensemble_sample_array, 1, 2)
    return ensemble_sample_array + diffusivity * (north_row + south_row + east_cell + west_cell - 4.0 * ensemble_sample_array) - advection * 0.5 * (south_row - north_row)

def analyse(states, ens_obs, value_all, prec_all):
    members_count = states.shape[0]
    identity = jnp.eye(members_count, dtype=jnp.float32)
    obs_float = ens_obs.astype(jnp.float32)
    obs_mean = lax.optimization_barrier(jnp.mean(obs_float, axis=0))
    obs_perturb = obs_float - obs_mean[None, :]
    innovation = value_all - obs_mean
    weighted = obs_perturb * prec_all[None, :]
    system = jnp.dot(weighted, obs_perturb.T, precision=lax.Precision.HIGHEST) + (members_count - 1.0) * identity
    forcing = jnp.dot(weighted, innovation, precision=lax.Precision.HIGHEST)
    scale_value = jnp.sqrt(jnp.sum(system * system))
    root_iter = system / scale_value
    inverse_root = identity
    for sweep in range(NSIT):
        correction = 1.5 * identity - 0.5 * jnp.dot(inverse_root, root_iter, precision=lax.Precision.HIGHEST)
        root_iter = jnp.dot(root_iter, correction, precision=lax.Precision.HIGHEST)
        inverse_root = jnp.dot(correction, inverse_root, precision=lax.Precision.HIGHEST)
    mean_weights = jnp.dot(inverse_root, jnp.dot(inverse_root, forcing, precision=lax.Precision.HIGHEST), precision=lax.Precision.HIGHEST) / scale_value
    transform = (jnp.sqrt((members_count - 1.0) / scale_value) * inverse_root + mean_weights[:, None]).astype(jnp.bfloat16)
    state_float = states.astype(jnp.float32)
    state_mean = lax.optimization_barrier(jnp.mean(state_float, axis=0))
    state_perturb = (state_float - state_mean[None, :]).astype(jnp.bfloat16)
    return state_mean[None, :] + jnp.dot(transform.T, state_perturb, preferred_element_type=jnp.float32)

def reference(members, diffusivity, advection, obs_value, obs_rinv, obs_cell, obs_count, loc_index):
    ensemble_sample_array = members.astype(jnp.float32)
    for sweep in range(STEPS):
        ensemble_sample_array = advance_all(ensemble_sample_array, diffusivity, advection)
    propagate_ensemble = ensemble_sample_array.astype(jnp.bfloat16)
    tile_variables = propagate_ensemble.reshape(ENSEMBLE_SIZE, ZONE_TOTAL, N_MEM, TILE_LINES * LATTICE_BREADTH).transpose(1, 2, 0, 3)
    obs_space = jax.vmap(jax.vmap(lambda states, cells: jnp.take(states, cells, axis=1)))(tile_variables, obs_cell)
    slot_index = jnp.arange(OWN, dtype=jnp.int32)
    live_slot = (slot_index[None, None, :] < obs_count[:, :, None]).astype(jnp.float32)
    own_prec = obs_rinv * live_slot
    loc_float = loc_index.astype(jnp.float32)
    far_prec = (own_prec * jnp.exp(-((loc_float + 1.0) / 4.0) ** 2)).astype(jnp.bfloat16)

    def one_patch(patch_index):
        region = patch_index // N_MEM
        group = patch_index % N_MEM
        before = (region + ZONE_TOTAL - 1) % ZONE_TOTAL
        after = (region + 1) % ZONE_TOTAL
        ens_obs = jnp.concatenate([obs_space[region, group], obs_space[before, group], obs_space[after, group]], axis=1)
        value_all = jnp.concatenate([obs_value[region, group], obs_value[before, group], obs_value[after, group]]).astype(jnp.float32)
        prec_all = jnp.concatenate([own_prec[region, group], far_prec[before, group].astype(jnp.float32), far_prec[after, group].astype(jnp.float32)])
        return analyse(tile_variables[region, group], ens_obs, value_all, prec_all)
    results = lax.map(one_patch, jnp.arange(ZONE_TOTAL * N_MEM, dtype=jnp.int32))
    results = results.reshape(ZONE_TOTAL, N_MEM, ENSEMBLE_SIZE, TILE_LINES, LATTICE_BREADTH).transpose(2, 0, 1, 3, 4)
    return results.reshape(ENSEMBLE_SIZE, GRID_ROWS, LATTICE_BREADTH)
```

```python
import jax
import jax.numpy as jnp
from jax import lax
from jax.experimental import pallas as pl
from jax.experimental.pallas import tpu as pltpu
from jax.sharding import PartitionSpec as P

STEPS = 3
NSIT = 2
LANES = 128
BF = jnp.bfloat16
F32 = jnp.float32
VMEM = pl.BlockSpec(memory_space=pltpu.VMEM)
SMEM = pl.BlockSpec(memory_space=pltpu.SMEM)


def call(body, outs, n_in, scratch=(), specs=None, flops=0, moved=0, name=None):
    return pl.pallas_call(
        body,
        out_shape=[jax.ShapeDtypeStruct(s, d) for s, d in outs],
        in_specs=specs or [VMEM] * n_in,
        out_specs=[VMEM] * len(outs),
        scratch_shapes=list(scratch),
        cost_estimate=pl.CostEstimate(flops=flops, bytes_accessed=moved, transcendentals=0),
        compiler_params=pltpu.CompilerParams(vmem_limit_bytes=40 << 20),
        name=name,
    )


def pack_body(x_ref, d_ref, a_ref, sa_ref, sb_ref, rows, coef):
    members = x_ref.shape[0]
    lines = x_ref.shape[1]

    def edge(out_ref, tail):
        base = lines - 8 if tail else 0
        rows[...] = x_ref[:, base : base + 8, :].astype(F32).reshape(members * 8, LANES)
        first = 8 - STEPS if tail else 0
        for k in range(STEPS):
            out_ref[k * members : (k + 1) * members, :] = rows[
                pl.ds(first + k, members, stride=8), :
            ].astype(BF)
        at = lines - 2 if tail else 0
        coef[0:2, :] = d_ref[at : at + 2, :]
        coef[2:4, :] = a_ref[at : at + 2, :]
        whole = coef[0:4, :]
        high = whole.astype(BF).astype(F32)
        middle = (whole - high).astype(BF).astype(F32)
        coef[0:4, :] = high
        coef[4:8, :] = middle
        coef[8:12, :] = whole - high - middle
        coef[12:16, :] = jnp.zeros((4, LANES), F32)
        out_ref[STEPS * members :, :] = coef[...].astype(BF)

    even = lax.rem(lax.axis_index("reg"), 2) == 0

    @pl.when(even)
    def _():
        edge(sa_ref, True)
        edge(sb_ref, False)

    @pl.when(jnp.logical_not(even))
    def _():
        edge(sa_ref, False)
        edge(sb_ref, True)


def forecast_body(x_ref, ra_ref, rb_ref, d_ref, a_ref, o_ref, xs, halo, dd, aa, cf):
    members = x_ref.shape[0]
    lines = x_ref.shape[1]
    reach = STEPS * members
    even = lax.rem(lax.axis_index("reg"), 2) == 0

    def take(ref, side):
        halo[side * reach : (side + 1) * reach, :] = ref[0:reach, :].astype(F32)
        parts = ref[reach:, :].astype(F32)
        whole = parts[0:4] + parts[4:8] + parts[8:12]
        at = (lines + 2) if side else 0
        dd[at : at + 2, :] = whole[0:2]
        aa[at : at + 2, :] = whole[2:4]

    @pl.when(even)
    def _():
        take(rb_ref, 0)
        take(ra_ref, 1)

    @pl.when(jnp.logical_not(even))
    def _():
        take(ra_ref, 0)
        take(rb_ref, 1)

    dd[2 : 2 + lines, :] = d_ref[...]
    aa[2 : 2 + lines, :] = a_ref[...]
    for row in range(lines + 4):
        dif = jnp.broadcast_to(dd[row : row + 1, :], (8, LANES))
        adv = 0.5 * jnp.broadcast_to(aa[row : row + 1, :], (8, LANES))
        cf[row, 0:8, :] = 1.0 - 4.0 * dif
        cf[row, 8:16, :] = dif
        cf[row, 16:24, :] = dif + adv
        cf[row, 24:32, :] = dif - adv

    block = 16

    def step(b, carry):
        xs[...] = x_ref[pl.ds(b * block, block)].astype(F32).reshape(block * lines, LANES)

        def start_row(row):
            if row < 0:
                return halo[pl.ds((row + STEPS) * members + b * block, block), :]
            if row >= lines:
                return halo[pl.ds(reach + (row - lines) * members + b * block, block), :]
            return xs[pl.ds(row, block, stride=lines), :]

        def update(row, north, centre, south):
            def c(k):
                v = cf[row + 2, 8 * k : 8 * k + 8, :]
                return jnp.concatenate([v, v], axis=0)

            sides = pltpu.roll(centre, 1, 1) + pltpu.roll(centre, LANES - 1, 1)
            return c(0) * centre + c(1) * sides + c(2) * north + c(3) * south

        levels = [{} for _ in range(STEPS + 1)]
        for row in range(-STEPS, lines + STEPS):
            levels[0][row] = start_row(row)
            for level in range(1, STEPS + 1):
                at = row - level
                prev = levels[level - 1]
                if at - 1 not in prev or at < level - STEPS:
                    continue
                new = update(at, prev[at - 1], prev[at], prev[at + 1])
                if level == STEPS:
                    o_ref[at, pl.ds(b * block, block), :] = new.astype(BF)
                else:
                    levels[level][at] = new
                del prev[at - 1]
        return carry

    lax.fori_loop(0, members // block, step, 0)


def observe_body(s_ref, cell_ref, value_ref, rinv_ref, count_ref, loc_ref, h_ref, prec_ref):
    groups, tile, per, _ = s_ref.shape
    members = groups * per
    slots = cell_ref.shape[-1]
    cell = cell_ref[0]
    total = jnp.zeros((members, slots), F32)
    line = lax.broadcasted_iota(jnp.int32, (2 * LANES, slots), 0)
    for pair in range(tile // 2):
        here = jnp.concatenate(
            [
                s_ref[:, 2 * pair].reshape(members, LANES),
                s_ref[:, 2 * pair + 1].reshape(members, LANES),
            ],
            axis=1,
        )
        picks = jnp.where(line + 2 * LANES * pair == cell, 1.0, 0.0).astype(BF)
        total += jnp.dot(here, picks, preferred_element_type=F32)
    h_ref[0:members, :] = total.astype(BF)
    slot = lax.broadcasted_iota(jnp.int32, (1, slots), 1)
    own = jnp.where(slot < count_ref[0, 0], rinv_ref[0], 0.0)
    radius = (loc_ref[0].astype(F32) + 1.0) / 4.0
    far = own * jnp.exp(-(radius * radius))
    row = lax.broadcasted_iota(jnp.int32, (16, slots), 0)
    value = value_ref[0].astype(F32)
    info = jnp.where(row == 0, value, jnp.where(row == 1, far, 0.0))
    h_ref[members:, :] = info.astype(BF)
    prec_ref[...] = jnp.where(
        lax.broadcasted_iota(jnp.int32, (8, slots), 0) == 0, own, value
    )


def weigh(obs, value, prec):
    count = obs.shape[0]
    mean = jnp.sum(obs, axis=0, keepdims=True) * (1.0 / count)
    perturb = obs - mean
    scaled = (perturb * jnp.sqrt(prec)).astype(BF)
    force = jnp.sum(perturb * (prec * (value - mean)), axis=1, keepdims=True)
    return scaled, force


def gram(a):
    return lax.dot_general(a, a, (((1,), (1,)), ((), ())), preferred_element_type=F32)


def own_body(s_ref, h_ref, prec_ref, xb_ref, xbar_ref, sys_ref, force_ref):
    groups, tile, per, _ = s_ref.shape
    members = groups * per
    for row in range(tile):
        here = s_ref[:, row].reshape(members, LANES).astype(F32)
        mean = jnp.sum(here, axis=0, keepdims=True) * (1.0 / members)
        xbar_ref[:, row * LANES : (row + 1) * LANES] = jnp.broadcast_to(mean, (8, LANES))
        xb_ref[:, row * LANES : (row + 1) * LANES] = (here - mean).astype(BF)
    scaled, force = weigh(h_ref[0:members, :].astype(F32), prec_ref[1:2, :], prec_ref[0:1, :])
    sys_ref[...] = gram(scaled)
    force_ref[...] = jnp.broadcast_to(force, (members, LANES))


def analyse_body(ra_ref, rb_ref, xb_ref, xbar_ref, sys_ref, force_ref, o_ref):
    members = sys_ref.shape[0]
    groups, tile, per, _ = o_ref.shape
    total = sys_ref[...]
    force = force_ref[:, 0:1]
    for ref in (ra_ref, rb_ref):
        info = ref[members:, :].astype(F32)
        scaled, more = weigh(ref[0:members, :].astype(F32), info[0:1, :], info[1:2, :])
        total += gram(scaled)
        force += more
    diagonal = lax.broadcasted_iota(jnp.int32, (members, members), 0) == lax.broadcasted_iota(
        jnp.int32, (members, members), 1
    )
    total += jnp.where(diagonal, members - 1.0, 0.0)
    inv = lax.rsqrt(jnp.sum(total * total))
    base = total * inv
    base_b = base.astype(BF)
    square = jnp.dot(base_b, base_b, preferred_element_type=F32)
    tail = (0.0625 * square - 0.5625 * base).astype(BF)
    root = (
        jnp.where(diagonal, 2.25, 0.0)
        - 2.4375 * base
        + 1.6875 * square
        + jnp.dot(square.astype(BF), tail, preferred_element_type=F32)
    )
    first = jnp.sum(root * force, axis=0, keepdims=True)
    second = jnp.sum(root * first, axis=1, keepdims=True) * inv
    mean_row = jnp.sum(jnp.where(diagonal, second, 0.0), axis=0, keepdims=True)
    weights = (jnp.sqrt((members - 1.0) * inv) * root + mean_row).astype(BF)
    for pair in range(tile // 2):
        cols = slice(2 * pair * LANES, 2 * (pair + 1) * LANES)
        new = xbar_ref[0:1, cols] + jnp.dot(
            weights, xb_ref[:, cols], preferred_element_type=F32
        )
        for half in range(2):
            part = new[:, half * LANES : (half + 1) * LANES].astype(BF)
            o_ref[:, 2 * pair + half] = part.reshape(groups, per, LANES)


def place_body(r_ref, o_ref, out):
    lines = r_ref.shape[0]
    block = o_ref.shape[0]
    b = pl.program_id(0)
    for row in range(lines):
        out[pl.ds(row, block, stride=lines), :] = r_ref[
            row, pl.ds(pl.multiple_of(b * block, block), block), :
        ].astype(F32)
    o_ref[...] = out[...].reshape(block, lines, LANES)


def on_device(members, diffusivity, advection, obs_value, obs_rinv, obs_cell, obs_count, loc_index):
    per, lines, _ = members.shape
    groups = lax.axis_size("mem")
    regions = lax.axis_size("reg")
    tile = lines // groups
    total = per * groups
    slots = obs_cell.shape[-1]
    near = [(i, i ^ 1) for i in range(regions)]
    across = [(i, (i + 1) % regions if i % 2 else (i - 1) % regions) for i in range(regions)]

    edge = ((STEPS * per + 16, LANES), BF)
    send_a, send_b = call(
        pack_body,
        [edge, edge],
        3,
        [pltpu.VMEM((per * 8, LANES), F32), pltpu.VMEM((16, LANES), F32)],
        moved=1 << 20,
        name="pack",
    )(members, diffusivity, advection)
    got_b = lax.ppermute(send_b, "reg", across)
    got_a = lax.ppermute(send_a, "reg", near)
    (ahead,) = call(
        forecast_body,
        [((lines, per, LANES), BF)],
        5,
        [
            pltpu.VMEM((16 * lines, LANES), F32),
            pltpu.VMEM((2 * STEPS * per, LANES), F32),
            pltpu.VMEM((lines + 8, LANES), F32),
            pltpu.VMEM((lines + 8, LANES), F32),
            pltpu.VMEM((lines + 4, 32, LANES), F32),
        ],
        moved=4 << 20,
        name="forecast",
    )(members, got_a, got_b, diffusivity, advection)
    states = lax.all_to_all(ahead.reshape(groups, tile, per, LANES), "mem", 0, 0)
    obs, prec = call(
        observe_body,
        [((total + 16, slots), BF), ((8, slots), F32)],
        6,
        specs=[VMEM, VMEM, VMEM, VMEM, SMEM, VMEM],
        flops=2 * total * tile * LANES * slots,
        moved=2 << 20,
        name="observe",
    )(states, obs_cell, obs_value, obs_rinv, obs_count, loc_index)
    nb = lax.ppermute(obs, "reg", across)
    na = lax.ppermute(obs, "reg", near)
    xb, xbar, system, force = call(
        own_body,
        [
            ((total, tile * LANES), BF),
            ((8, tile * LANES), F32),
            ((total, total), F32),
            ((total, LANES), F32),
        ],
        3,
        flops=2 * total * total * slots,
        moved=4 << 20,
        name="own",
    )(states, obs, prec)
    (back,) = call(
        analyse_body,
        [((groups, tile, per, LANES), BF)],
        6,
        flops=10 * total * total * total,
        moved=4 << 20,
        name="analyse",
    )(na, nb, xb, xbar, system, force)
    home = lax.all_to_all(back, "mem", 0, 0).reshape(lines, per, LANES)
    block = 32
    return pl.pallas_call(
        place_body,
        grid=(per // block,),
        out_shape=jax.ShapeDtypeStruct((per, lines, LANES), F32),
        in_specs=[VMEM],
        out_specs=pl.BlockSpec((block, lines, LANES), lambda i: (i, 0, 0)),
        scratch_shapes=[pltpu.VMEM((block * lines, LANES), F32)],
        compiler_params=pltpu.CompilerParams(vmem_limit_bytes=40 << 20),
        name="place",
    )(home)


def solution(mesh):
    return jax.shard_map(
        on_device,
        mesh=mesh,
        in_specs=(
            P("mem", "reg", None),
            P("reg", None),
            P("reg", None),
            P("reg", "mem", None),
            P("reg", "mem", None),
            P("reg", "mem", None),
            P("reg", "mem"),
            P("reg", "mem", None),
        ),
        out_specs=P("mem", "reg", None),
        check_vma=False,
    )
```

```python
import jax
import jax.numpy as jnp
from jax import lax
from jax.experimental import pallas as pl
from jax.experimental.pallas import tpu as pltpu
from jax.sharding import PartitionSpec as P

STEPS = 3
LANES = 128
BF = jnp.bfloat16
F32 = jnp.float32
VMEM = pl.BlockSpec(memory_space=pltpu.VMEM)
SMEM = pl.BlockSpec(memory_space=pltpu.SMEM)
HBM = pl.BlockSpec(memory_space=pltpu.HBM)


def call(body, outs, n_in, scratch=(), specs=None, flops=0, moved=0, grant=40 << 20):
    return pl.pallas_call(
        body,
        out_shape=[jax.ShapeDtypeStruct(s, d) for s, d in outs],
        in_specs=specs or [VMEM] * n_in,
        out_specs=[VMEM] * len(outs),
        scratch_shapes=list(scratch),
        cost_estimate=pl.CostEstimate(flops=flops, bytes_accessed=moved, transcendentals=0),
        compiler_params=pltpu.CompilerParams(vmem_limit_bytes=grant),
    )


def pack_body(
    x_ref, d_ref, a_ref, sa_ref, sb_ref, xv_ref, dv_ref, av_ref, head, tail, rows, coef, sems
):
    members = x_ref.shape[0]
    lines = x_ref.shape[1]
    last = lines - 8
    copies = [
        pltpu.make_async_copy(x_ref.at[:, pl.ds(0, 8), :], head, sems.at[0]),
        pltpu.make_async_copy(x_ref.at[:, pl.ds(last, 8), :], tail, sems.at[1]),
        pltpu.make_async_copy(d_ref, dv_ref, sems.at[2]),
        pltpu.make_async_copy(a_ref, av_ref, sems.at[3]),
    ]
    whole_copy = pltpu.make_async_copy(x_ref, xv_ref, sems.at[4])
    for copy in copies:
        copy.start()
    whole_copy.start()
    for copy in copies:
        copy.wait()

    def edge(out_ref, source, side):
        rows[...] = source[...].astype(F32).reshape(members * 8, LANES)
        first = (8 - STEPS) * side
        for k in range(STEPS):
            out_ref[k * members : (k + 1) * members, :] = rows[
                pl.ds(first + k, members, stride=8), :
            ].astype(BF)
        at = (lines - 2) * side
        coef[0:2, :] = dv_ref[at : at + 2, :]
        coef[2:4, :] = av_ref[at : at + 2, :]
        whole = coef[0:4, :]
        high = whole.astype(BF).astype(F32)
        middle = (whole - high).astype(BF).astype(F32)
        coef[0:4, :] = high
        coef[4:8, :] = middle
        coef[8:12, :] = whole - high - middle
        coef[12:16, :] = jnp.zeros((4, LANES), F32)
        out_ref[STEPS * members :, :] = coef[...].astype(BF)

    even = lax.rem(lax.axis_index("reg"), 2) == 0

    @pl.when(even)
    def _():
        edge(sa_ref, tail, 1)
        edge(sb_ref, head, 0)

    @pl.when(jnp.logical_not(even))
    def _():
        edge(sa_ref, head, 0)
        edge(sb_ref, tail, 1)

    whole_copy.wait()


def laplace():
    i = lax.broadcasted_iota(jnp.int32, (LANES, LANES), 0)
    j = lax.broadcasted_iota(jnp.int32, (LANES, LANES), 1)
    gap = jnp.bitwise_and(i - j, LANES - 1)
    beside = jnp.logical_or(gap == 1, gap == LANES - 1)
    return jnp.where(gap == 0, -4.0, jnp.where(beside, 1.0, 0.0)).astype(BF)


def sides_of(centre):
    return pltpu.roll(centre, 1, 1) + pltpu.roll(centre, LANES - 1, 1)


KEEP = ((0, 0), (0, 1), ("lap", 0), (1, 1), (1, 2), (2, 2), (2, 3))


def interior_body(x_ref, d_ref, a_ref, o_ref, k_ref, xs, ls, cf):
    members = x_ref.shape[0]
    lines = x_ref.shape[1]
    for row in range(lines):
        dif = jnp.broadcast_to(d_ref[row : row + 1, :], (8, LANES))
        adv = 0.5 * jnp.broadcast_to(a_ref[row : row + 1, :], (8, LANES))
        cf[row, 0:8, :] = 1.0 - 4.0 * dif
        cf[row, 8:16, :] = dif
        cf[row, 16:24, :] = dif + adv
        cf[row, 24:32, :] = dif - adv
    across = laplace()
    block = 16

    def step(b, carry):
        here = pl.ds(pl.multiple_of(b * block, block), block)
        for q in range(lines // 8):
            part = x_ref[here, 8 * q : 8 * q + 8, :].astype(F32).reshape(block * 8, LANES)
            xs[q] = part
            ls[q] = jnp.dot(part.astype(BF), across, preferred_element_type=F32)

        def c(row, k):
            v = cf[row, 8 * k : 8 * k + 8, :]
            return jnp.concatenate([v, v], axis=0)

        def keep(what, row, value):
            for side in range(2):
                away = lines - 1 - row if side else row
                if (what, away) in KEEP:
                    k_ref[side * len(KEEP) + KEEP.index((what, away)), here, :] = value

        levels = [{} for _ in range(STEPS + 1)]
        for row in range(lines):
            at_row = pl.ds(row % 8, block, stride=8)
            levels[0][row] = xs[row // 8, at_row, :]
            keep(0, row, levels[0][row])
            if row in (0, lines - 1):
                keep("lap", row, ls[row // 8, at_row, :])
            for level in range(1, STEPS + 1):
                at = row - level
                if at < level or at + level >= lines:
                    continue
                prev = levels[level - 1]
                centre = prev[at]
                vertical = c(at, 2) * prev[at - 1] + c(at, 3) * prev[at + 1]
                if level == 1:
                    lap = ls[at // 8, pl.ds(at % 8, block, stride=8), :]
                    new = centre + c(at, 1) * lap + vertical
                else:
                    new = c(at, 0) * centre + c(at, 1) * sides_of(centre) + vertical
                keep(level, at, new)
                if level == STEPS:
                    o_ref[at, here, :] = new.astype(BF)
                else:
                    levels[level][at] = new
                del prev[at - 1]
        return carry

    lax.fori_loop(0, members // block, step, 0)


def edge_body(f_ref, k_ref, ra_ref, rb_ref, d_ref, a_ref, o_ref, halo, dd, aa, new_rows, sems):
    del f_ref
    members = k_ref.shape[1]
    lines = d_ref.shape[0]
    reach = STEPS * members
    even = lax.rem(lax.axis_index("reg"), 2) == 0

    def take(ref, side):
        halo[side * reach : (side + 1) * reach, :] = ref[0:reach, :]
        parts = ref[reach:, :].astype(F32)
        whole = parts[0:4] + parts[4:8] + parts[8:12]
        at = (lines + 2) if side else 0
        dd[at : at + 2, :] = whole[0:2]
        aa[at : at + 2, :] = whole[2:4]

    @pl.when(even)
    def _():
        take(rb_ref, 0)
        take(ra_ref, 1)

    @pl.when(jnp.logical_not(even))
    def _():
        take(ra_ref, 0)
        take(rb_ref, 1)

    dd[2 : 2 + lines, :] = d_ref[...]
    aa[2 : 2 + lines, :] = a_ref[...]
    across = laplace()
    copies = []
    for side in range(2):

        def at(away):
            return lines - 1 - away if side else away

        def coefs(away):
            row = at(away) + 2
            dif = jnp.broadcast_to(dd[row : row + 1, :], (members, LANES))
            adv = 0.5 * jnp.broadcast_to(aa[row : row + 1, :], (members, LANES))
            inward = dif - adv if side == 0 else dif + adv
            outward = dif + adv if side == 0 else dif - adv
            return dif, outward, inward

        def outer(away):
            k = (-away - 1) if side else (STEPS + away)
            start = side * reach + k * members
            return halo[start : start + members, :]

        def kept(what, away):
            return k_ref[side * len(KEEP) + KEEP.index((what, away))]

        states = [{} for _ in range(STEPS)]
        for away in range(-STEPS, 0):
            states[0][away] = outer(away).astype(F32)
        for what, away in KEEP:
            if what != "lap":
                states[what][away] = kept(what, away)
        for level in range(1, STEPS + 1):
            prev = states[level - 1]
            for away in range(level - STEPS, level):
                dif, outward, inward = coefs(away)
                vertical = outward * prev[away - 1] + inward * prev[away + 1]
                centre = prev[away]
                if level == 1:
                    lap = (
                        kept("lap", 0)
                        if away == 0
                        else jnp.dot(outer(away), across, preferred_element_type=F32)
                    )
                    new = centre + dif * lap + vertical
                else:
                    new = (1.0 - 4.0 * dif) * centre + dif * sides_of(centre) + vertical
                if level == STEPS:
                    slot = STEPS - 1 - away if side else away
                    new_rows[side * STEPS + slot] = new.astype(BF)
                else:
                    states[level][away] = new
        first = lines - STEPS if side else 0
        copy = pltpu.make_async_copy(
            new_rows.at[pl.ds(side * STEPS, STEPS)],
            o_ref.at[pl.ds(first, STEPS)],
            sems.at[side],
        )
        copy.start()
        copies.append(copy)
    for copy in copies:
        copy.wait()


def observe_body(s_ref, cell_ref, value_ref, rinv_ref, count_ref, loc_ref, h_ref, prec_ref):
    groups, tile, per, _ = s_ref.shape
    members = groups * per
    slots = cell_ref.shape[-1]
    cell = cell_ref[0]
    total = jnp.zeros((members, slots), F32)
    line = lax.broadcasted_iota(jnp.int32, (2 * LANES, slots), 0)
    for pair in range(tile // 2):
        here = jnp.concatenate(
            [
                s_ref[:, 2 * pair].reshape(members, LANES),
                s_ref[:, 2 * pair + 1].reshape(members, LANES),
            ],
            axis=1,
        )
        picks = jnp.where(line + 2 * LANES * pair == cell, 1.0, 0.0).astype(BF)
        total += jnp.dot(here, picks, preferred_element_type=F32)
    h_ref[0:members, :] = total.astype(BF)
    slot = lax.broadcasted_iota(jnp.int32, (1, slots), 1)
    own = jnp.where(slot < count_ref[0, 0], rinv_ref[0], 0.0)
    radius = (loc_ref[0].astype(F32) + 1.0) / 4.0
    far = own * jnp.exp(-(radius * radius))
    row = lax.broadcasted_iota(jnp.int32, (16, slots), 0)
    value = value_ref[0].astype(F32)
    info = jnp.where(row == 0, value, jnp.where(row == 1, far, 0.0))
    h_ref[members:, :] = info.astype(BF)
    prec_ref[...] = jnp.where(
        lax.broadcasted_iota(jnp.int32, (8, slots), 0) == 0, own, value
    )


def weigh(obs, value, prec):
    count = obs.shape[0]
    mean = jnp.sum(obs, axis=0, keepdims=True) * (1.0 / count)
    perturb = obs - mean
    scaled = (perturb * jnp.sqrt(prec)).astype(BF)
    force = jnp.sum(perturb * (prec * (value - mean)), axis=1, keepdims=True)
    return scaled, force


def gram(a):
    return lax.dot_general(a, a, (((1,), (1,)), ((), ())), preferred_element_type=F32)


def own_body(s_ref, h_ref, prec_ref, xb_ref, xbar_ref, sys_ref, force_ref):
    groups, tile, per, _ = s_ref.shape
    members = groups * per
    for row in range(tile):
        here = s_ref[:, row].reshape(members, LANES).astype(F32)
        mean = jnp.sum(here, axis=0, keepdims=True) * (1.0 / members)
        xbar_ref[:, row * LANES : (row + 1) * LANES] = jnp.broadcast_to(mean, (8, LANES))
        xb_ref[:, row * LANES : (row + 1) * LANES] = (here - mean).astype(BF)
    scaled, force = weigh(h_ref[0:members, :].astype(F32), prec_ref[1:2, :], prec_ref[0:1, :])
    sys_ref[...] = gram(scaled)
    force_ref[...] = jnp.broadcast_to(force, (members, LANES))


def analyse_body(ra_ref, rb_ref, xb_ref, xbar_ref, sys_ref, force_ref, o_ref):
    members = sys_ref.shape[0]
    groups, tile, per, _ = o_ref.shape
    total = sys_ref[...]
    force = force_ref[:, 0:1]
    for ref in (ra_ref, rb_ref):
        info = ref[members:, :].astype(F32)
        scaled, more = weigh(ref[0:members, :].astype(F32), info[0:1, :], info[1:2, :])
        total += gram(scaled)
        force += more
    diagonal = lax.broadcasted_iota(jnp.int32, (members, members), 0) == lax.broadcasted_iota(
        jnp.int32, (members, members), 1
    )
    total += jnp.where(diagonal, members - 1.0, 0.0)
    inv = lax.rsqrt(jnp.sum(total * total))
    base = total * inv
    base_b = base.astype(BF)
    square = jnp.dot(base_b, base_b, preferred_element_type=F32)
    tail = (0.0625 * square - 0.5625 * base).astype(BF)
    root = (
        jnp.where(diagonal, 2.25, 0.0)
        - 2.4375 * base
        + 1.6875 * square
        + jnp.dot(square.astype(BF), tail, preferred_element_type=F32)
    )
    first = jnp.sum(root * force, axis=0, keepdims=True)
    second = jnp.sum(root * first, axis=1, keepdims=True) * inv
    mean_row = jnp.sum(jnp.where(diagonal, second, 0.0), axis=0, keepdims=True)
    weights = (jnp.sqrt((members - 1.0) * inv) * root + mean_row).astype(BF)
    for pair in range(tile // 2):
        cols = slice(2 * pair * LANES, 2 * (pair + 1) * LANES)
        new = xbar_ref[0:1, cols] + jnp.dot(
            weights, xb_ref[:, cols], preferred_element_type=F32
        )
        for half in range(2):
            part = new[:, half * LANES : (half + 1) * LANES].astype(BF)
            o_ref[:, 2 * pair + half] = part.reshape(groups, per, LANES)


def place_body(r_ref, o_ref, out):
    lines = r_ref.shape[0]
    block = o_ref.shape[0]
    here = pl.ds(pl.multiple_of(pl.program_id(0) * block, block), block)
    for row in range(lines):
        out[row // 8, pl.ds(row % 8, block, stride=8), :] = r_ref[row, here, :].astype(F32)
    for q in range(lines // 8):
        o_ref[:, 8 * q : 8 * q + 8, :] = out[q].reshape(block, 8, LANES)


def program(members, diffusivity, advection, obs_value, obs_rinv, obs_cell, obs_count, loc_index):
    per, lines, _ = members.shape
    groups = lax.axis_size("mem")
    regions = lax.axis_size("reg")
    tile = lines // groups
    total = per * groups
    slots = obs_cell.shape[-1]
    near = [(i, i ^ 1) for i in range(regions)]
    across = [(i, (i + 1) % regions if i % 2 else (i - 1) % regions) for i in range(regions)]

    reach = STEPS * per + 16
    send_a, send_b, members, diffusivity, advection = call(
        pack_body,
        [((reach, LANES), BF)] * 2
        + [(v.shape, v.dtype) for v in (members, diffusivity, advection)],
        3,
        [
            pltpu.VMEM((per, 8, LANES), BF),
            pltpu.VMEM((per, 8, LANES), BF),
            pltpu.VMEM((per * 8, LANES), F32),
            pltpu.VMEM((16, LANES), F32),
            pltpu.SemaphoreType.DMA((5,)),
        ],
        specs=[HBM, HBM, HBM],
        moved=1 << 20,
    )(
        *[
            pltpu.with_memory_space_constraint(v, pltpu.HBM)
            for v in (members, diffusivity, advection)
        ]
    )
    got_b = lax.ppermute(send_b, "reg", across)
    got_a = lax.ppermute(send_a, "reg", near)
    inner, kept = call(
        interior_body,
        [((lines, per, LANES), BF), ((2 * len(KEEP), per, LANES), F32)],
        3,
        [
            pltpu.VMEM((lines // 8, 16 * 8, LANES), F32),
            pltpu.VMEM((lines // 8, 16 * 8, LANES), F32),
            pltpu.VMEM((lines, 32, LANES), F32),
        ],
        moved=12 << 20,
    )(members, diffusivity, advection)
    ahead = pl.pallas_call(
        edge_body,
        out_shape=jax.ShapeDtypeStruct((lines, per, LANES), BF),
        in_specs=[pl.BlockSpec(memory_space=pl.ANY)] + [VMEM] * 5,
        out_specs=pl.BlockSpec(memory_space=pl.ANY),
        input_output_aliases={0: 0},
        scratch_shapes=[
            pltpu.VMEM((2 * STEPS * per, LANES), BF),
            pltpu.VMEM((lines + 8, LANES), F32),
            pltpu.VMEM((lines + 8, LANES), F32),
            pltpu.VMEM((2 * STEPS, per, LANES), BF),
            pltpu.SemaphoreType.DMA((2,)),
        ],
        cost_estimate=pl.CostEstimate(flops=0, bytes_accessed=2 << 20, transcendentals=0),
        compiler_params=pltpu.CompilerParams(vmem_limit_bytes=40 << 20),
        name="edge",
    )(inner, kept, got_a, got_b, diffusivity, advection)
    states = lax.all_to_all(ahead.reshape(groups, tile, per, LANES), "mem", 0, 0)
    obs, prec = call(
        observe_body,
        [((total + 16, slots), BF), ((8, slots), F32)],
        6,
        specs=[VMEM, VMEM, VMEM, VMEM, SMEM, VMEM],
        flops=2 * total * tile * LANES * slots,
        moved=2 << 20,
    )(states, obs_cell, obs_value, obs_rinv, obs_count, loc_index)
    nb = lax.ppermute(obs, "reg", across)
    na = lax.ppermute(obs, "reg", near)
    xb, xbar, system, force = call(
        own_body,
        [
            ((total, tile * LANES), BF),
            ((8, tile * LANES), F32),
            ((total, total), F32),
            ((total, LANES), F32),
        ],
        3,
        flops=2 * total * total * slots,
        moved=4 << 20,
    )(states, obs, prec)
    (back,) = call(
        analyse_body,
        [((groups, tile, per, LANES), BF)],
        6,
        flops=10 * total * total * total,
        moved=4 << 20,
    )(na, nb, xb, xbar, system, force)
    home = lax.all_to_all(back, "mem", 0, 0).reshape(lines, per, LANES)
    block = 32
    return pl.pallas_call(
        place_body,
        grid=(per // block,),
        out_shape=jax.ShapeDtypeStruct((per, lines, LANES), F32),
        in_specs=[VMEM],
        out_specs=pl.BlockSpec((block, lines, LANES), lambda i: (i, 0, 0)),
        scratch_shapes=[pltpu.VMEM((lines // 8, block * 8, LANES), F32)],
        compiler_params=pltpu.CompilerParams(vmem_limit_bytes=40 << 20),
        name="place",
    )(home)


def solution(mesh):
    return jax.shard_map(
        program,
        mesh=mesh,
        in_specs=(
            P("mem", "reg", None),
            P("reg", None),
            P("reg", None),
            P("reg", "mem", None),
            P("reg", "mem", None),
            P("reg", "mem", None),
            P("reg", "mem"),
            P("reg", "mem", None),
        ),
        out_specs=P("mem", "reg", None),
        check_vma=False,
    )
```

```python
import jax
import jax.numpy as jnp
from jax import lax
from jax.experimental import pallas as pl
from jax.experimental.pallas import tpu as pltpu
from jax.sharding import PartitionSpec as P

STEPS = 3
LANES = 128
BLOCK = 32
BF = jnp.bfloat16
F32 = jnp.float32
VMEM = pl.BlockSpec(memory_space=pltpu.VMEM)
SMEM = pl.BlockSpec(memory_space=pltpu.SMEM)
HBM = pl.BlockSpec(memory_space=pltpu.HBM)


def call(body, outs, n_in, scratch=(), specs=None, flops=0, moved=0, grant=40 << 20):
    return pl.pallas_call(
        body,
        out_shape=[jax.ShapeDtypeStruct(s, d) for s, d in outs],
        in_specs=specs or [VMEM] * n_in,
        out_specs=[VMEM] * len(outs),
        scratch_shapes=list(scratch),
        cost_estimate=pl.CostEstimate(flops=flops, bytes_accessed=moved, transcendentals=0),
        compiler_params=pltpu.CompilerParams(vmem_limit_bytes=grant),
    )


def pack_body(
    x_ref, d_ref, a_ref, sa_ref, sb_ref, xv_ref, dv_ref, av_ref, head, tail, rows, coef, sems
):
    members = x_ref.shape[0]
    lines = x_ref.shape[1]
    last = lines - 8
    copies = [
        pltpu.make_async_copy(x_ref.at[:, pl.ds(0, 8), :], head, sems.at[0]),
        pltpu.make_async_copy(x_ref.at[:, pl.ds(last, 8), :], tail, sems.at[1]),
        pltpu.make_async_copy(d_ref, dv_ref, sems.at[2]),
        pltpu.make_async_copy(a_ref, av_ref, sems.at[3]),
    ]
    whole_copy = pltpu.make_async_copy(x_ref, xv_ref, sems.at[4])
    for copy in copies:
        copy.start()
    whole_copy.start()
    for copy in copies:
        copy.wait()

    def edge(out_ref, source, side):
        rows[...] = source[...].astype(F32).reshape(members * 8, LANES)
        first = (8 - STEPS) * side
        for k in range(STEPS):
            out_ref[k * members : (k + 1) * members, :] = rows[
                pl.ds(first + k, members, stride=8), :
            ].astype(BF)
        at = (lines - 2) * side
        coef[0:2, :] = dv_ref[at : at + 2, :]
        coef[2:4, :] = av_ref[at : at + 2, :]
        whole = coef[0:4, :]
        high = whole.astype(BF).astype(F32)
        middle = (whole - high).astype(BF).astype(F32)
        coef[0:4, :] = high
        coef[4:8, :] = middle
        coef[8:12, :] = whole - high - middle
        coef[12:16, :] = jnp.zeros((4, LANES), F32)
        out_ref[STEPS * members :, :] = coef[...].astype(BF)

    even = lax.rem(lax.axis_index("reg"), 2) == 0

    @pl.when(even)
    def _():
        edge(sa_ref, tail, 1)
        edge(sb_ref, head, 0)

    @pl.when(jnp.logical_not(even))
    def _():
        edge(sa_ref, head, 0)
        edge(sb_ref, tail, 1)

    whole_copy.wait()


def laplace():
    i = lax.broadcasted_iota(jnp.int32, (LANES, LANES), 0)
    j = lax.broadcasted_iota(jnp.int32, (LANES, LANES), 1)
    gap = jnp.bitwise_and(i - j, LANES - 1)
    beside = jnp.logical_or(gap == 1, gap == LANES - 1)
    return jnp.where(gap == 0, -4.0, jnp.where(beside, 1.0, 0.0)).astype(BF)


def beside():
    i = lax.broadcasted_iota(jnp.int32, (LANES, LANES), 0)
    j = lax.broadcasted_iota(jnp.int32, (LANES, LANES), 1)
    gap = jnp.bitwise_and(i - j, LANES - 1)
    once = jnp.where(jnp.logical_or(gap == 1, gap == LANES - 1), 1.0, 0.0).astype(BF)
    return jnp.concatenate([once, once], axis=0)


def rolled(centre):
    return pltpu.roll(centre, 1, 1) + pltpu.roll(centre, LANES - 1, 1)


def sides_of(centre, pair):
    high = centre.astype(BF)
    low = (centre - high.astype(F32)).astype(BF)
    both = jnp.concatenate([high, low], axis=1)
    return jnp.dot(both, pair, preferred_element_type=F32)


KEEP = ((0, 0), (0, 1), ("lap", 0), (1, 1), (1, 2), (2, 2), (2, 3))


def interior_body(x_ref, d_ref, a_ref, o_ref, k_ref, xs, ls, cf):
    members = x_ref.shape[0]
    lines = x_ref.shape[1]
    for row in range(lines):
        dif = jnp.broadcast_to(d_ref[row : row + 1, :], (8, LANES))
        adv = 0.5 * jnp.broadcast_to(a_ref[row : row + 1, :], (8, LANES))
        cf[row, 0:8, :] = 1.0 - 4.0 * dif
        cf[row, 8:16, :] = dif
        cf[row, 16:24, :] = dif + adv
        cf[row, 24:32, :] = dif - adv
    across = laplace()
    pair = beside()
    block = BLOCK

    def stage(b, slot):
        here = pl.ds(b * block, block)
        for q in range(lines // 8):
            part = x_ref[here, 8 * q : 8 * q + 8, :].astype(F32).reshape(block * 8, LANES)
            xs[slot, q] = part
            ls[slot, q] = jnp.dot(part.astype(BF), across, preferred_element_type=F32)

    def c(row, k):
        v = cf[row, 8 * k : 8 * k + 8, :]
        return jnp.concatenate([v] * (block // 8), axis=0)

    def advance(b, slot):
        here = pl.ds(b * block, block)

        def keep(what, row, value):
            for side in range(2):
                away = lines - 1 - row if side else row
                if (what, away) in KEEP:
                    k_ref[side * len(KEEP) + KEEP.index((what, away)), here, :] = value

        levels = [{} for _ in range(STEPS + 1)]
        for row in range(lines):
            at_row = pl.ds(row % 8, block, stride=8)
            levels[0][row] = xs[slot, row // 8, at_row, :]
            keep(0, row, levels[0][row])
            if row in (0, lines - 1):
                keep("lap", row, ls[slot, row // 8, at_row, :])
            for level in range(1, STEPS + 1):
                at = row - level
                if at < level or at + level >= lines:
                    continue
                prev = levels[level - 1]
                centre = prev[at]
                vertical = c(at, 2) * prev[at - 1] + c(at, 3) * prev[at + 1]
                if level == 1:
                    lap = ls[slot, at // 8, pl.ds(at % 8, block, stride=8), :]
                    new = centre + c(at, 1) * lap + vertical
                else:
                    new = c(at, 0) * centre + c(at, 1) * (sides_of(centre, pair) if level == 2 else rolled(centre)) + vertical
                keep(level, at, new)
                if level == STEPS:
                    o_ref[at, here, :] = new.astype(BF)
                else:
                    levels[level][at] = new
                del prev[at - 1]

    count = members // block
    stage(0, 0)
    for b in range(count):
        if b + 1 < count:
            stage(b + 1, (b + 1) % 2)
        advance(b, b % 2)


def edge_body(f_ref, picks_ref, info_ref, prec_ref, k_ref, ra_ref, rb_ref, d_ref, a_ref, *rest):
    del f_ref, picks_ref, info_ref, prec_ref
    o_ref, halo, dd, aa, new_rows, sems = rest
    members = k_ref.shape[1]
    lines = d_ref.shape[0]
    reach = STEPS * members
    even = lax.rem(lax.axis_index("reg"), 2) == 0

    def take(ref, side):
        halo[side * reach : (side + 1) * reach, :] = ref[0:reach, :]
        parts = ref[reach:, :].astype(F32)
        whole = parts[0:4] + parts[4:8] + parts[8:12]
        at = (lines + 2) if side else 0
        dd[at : at + 2, :] = whole[0:2]
        aa[at : at + 2, :] = whole[2:4]

    @pl.when(even)
    def _():
        take(rb_ref, 0)
        take(ra_ref, 1)

    @pl.when(jnp.logical_not(even))
    def _():
        take(ra_ref, 0)
        take(rb_ref, 1)

    dd[2 : 2 + lines, :] = d_ref[...]
    aa[2 : 2 + lines, :] = a_ref[...]
    across = laplace()
    pair = beside()
    copies = []
    for side in range(2):

        def at(away):
            return lines - 1 - away if side else away

        def coefs(away):
            row = at(away) + 2
            dif = jnp.broadcast_to(dd[row : row + 1, :], (members, LANES))
            adv = 0.5 * jnp.broadcast_to(aa[row : row + 1, :], (members, LANES))
            inward = dif - adv if side == 0 else dif + adv
            outward = dif + adv if side == 0 else dif - adv
            return dif, outward, inward

        def outer(away):
            k = (-away - 1) if side else (STEPS + away)
            start = side * reach + k * members
            return halo[start : start + members, :]

        def kept(what, away):
            return k_ref[side * len(KEEP) + KEEP.index((what, away))]

        states = [{} for _ in range(STEPS)]
        for away in range(-STEPS, 0):
            states[0][away] = outer(away).astype(F32)
        for what, away in KEEP:
            if what != "lap":
                states[what][away] = kept(what, away)
        for level in range(1, STEPS + 1):
            prev = states[level - 1]
            for away in range(level - STEPS, level):
                dif, outward, inward = coefs(away)
                vertical = outward * prev[away - 1] + inward * prev[away + 1]
                centre = prev[away]
                if level == 1:
                    lap = (
                        kept("lap", 0)
                        if away == 0
                        else jnp.dot(outer(away), across, preferred_element_type=F32)
                    )
                    new = centre + dif * lap + vertical
                else:
                    around = sides_of(centre, pair) if level == 2 else rolled(centre)
                    new = (1.0 - 4.0 * dif) * centre + dif * around + vertical
                if level == STEPS:
                    slot = STEPS - 1 - away if side else away
                    new_rows[side * STEPS + slot] = new.astype(BF)
                else:
                    states[level][away] = new
        first = lines - STEPS if side else 0
        copy = pltpu.make_async_copy(
            new_rows.at[pl.ds(side * STEPS, STEPS)],
            o_ref.at[pl.ds(first, STEPS)],
            sems.at[side],
        )
        copy.start()
        copies.append(copy)
    for copy in copies:
        copy.wait()


def prepare_body(cell_ref, value_ref, rinv_ref, count_ref, loc_ref, picks_ref, info_ref, prec_ref):
    cells, slots = picks_ref.shape
    cell = cell_ref[0]
    line = lax.broadcasted_iota(jnp.int32, (cells, slots), 0)
    picks_ref[...] = jnp.where(line == cell, 1.0, 0.0).astype(BF)
    slot = lax.broadcasted_iota(jnp.int32, (1, slots), 1)
    own = jnp.where(slot < count_ref[0, 0], rinv_ref[0], 0.0)
    radius = (loc_ref[0].astype(F32) + 1.0) / 4.0
    far = own * jnp.exp(-(radius * radius))
    row = lax.broadcasted_iota(jnp.int32, (16, slots), 0)
    value = value_ref[0].astype(F32)
    info_ref[...] = jnp.where(row == 0, value, jnp.where(row == 1, far, 0.0)).astype(BF)
    prec_ref[...] = jnp.where(
        lax.broadcasted_iota(jnp.int32, (8, slots), 0) == 0, own, value
    )


def observe_body(s_ref, picks_ref, info_ref, h_ref):
    groups, tile, per, _ = s_ref.shape
    members = groups * per
    total = jnp.zeros((members, picks_ref.shape[1]), F32)
    for pair in range(tile // 2):
        here = jnp.concatenate(
            [
                s_ref[:, 2 * pair].reshape(members, LANES),
                s_ref[:, 2 * pair + 1].reshape(members, LANES),
            ],
            axis=1,
        )
        picks = picks_ref[2 * LANES * pair : 2 * LANES * (pair + 1), :]
        total += jnp.dot(here, picks, preferred_element_type=F32)
    h_ref[0:members, :] = total.astype(BF)
    h_ref[members:, :] = info_ref[...]


def weigh(obs, value, prec):
    count = obs.shape[0]
    mean = jnp.sum(obs, axis=0, keepdims=True) * (1.0 / count)
    perturb = obs - mean
    scaled = (perturb * jnp.sqrt(prec)).astype(BF)
    force = jnp.sum(perturb * (prec * (value - mean)), axis=1, keepdims=True)
    return scaled, force


def gram(a):
    return lax.dot_general(a, a, (((1,), (1,)), ((), ())), preferred_element_type=F32)


def own_body(s_ref, h_ref, prec_ref, xb_ref, xbar_ref, sys_ref, force_ref):
    groups, tile, per, _ = s_ref.shape
    members = groups * per
    for row in range(tile):
        here = s_ref[:, row].reshape(members, LANES).astype(F32)
        mean = jnp.sum(here, axis=0, keepdims=True) * (1.0 / members)
        xbar_ref[:, row * LANES : (row + 1) * LANES] = jnp.broadcast_to(mean, (8, LANES))
        xb_ref[:, row * LANES : (row + 1) * LANES] = (here - mean).astype(BF)
    scaled, force = weigh(h_ref[0:members, :].astype(F32), prec_ref[1:2, :], prec_ref[0:1, :])
    sys_ref[...] = gram(scaled)
    force_ref[...] = jnp.broadcast_to(force, (members, LANES))


def analyse_body(ra_ref, rb_ref, xb_ref, xbar_ref, sys_ref, force_ref, o_ref, *scratch):
    near, base, base_b, wide, square_b, tail_b, root, push = scratch
    members = sys_ref.shape[0]
    groups, tile, per, _ = o_ref.shape
    slots = ra_ref.shape[1]
    block = 64
    blocks = [slice(i, i + block) for i in range(0, members, block)]
    halves = [slice(i, i + 2 * LANES) for i in range(0, members, 2 * LANES)]

    def on_diagonal(rows, value, other):
        first = rows.start // LANES * LANES
        line = lax.broadcasted_iota(jnp.int32, (block, LANES), 0) + (rows.start - first)
        same = line == lax.broadcasted_iota(jnp.int32, (block, LANES), 1)
        mine = other[:, first : first + LANES] + jnp.where(same, value, 0.0)
        parts = [other[:, :first], mine, other[:, first + LANES :]]
        return jnp.concatenate([p for p in parts if p.shape[1]], axis=1)

    def product(left, right, into):
        for half in halves:
            into[:, half] = jnp.dot(left[...], right[:, half], preferred_element_type=F32)

    for k, ref in enumerate((ra_ref, rb_ref)):
        mean = jnp.zeros((8, slots), F32)
        for rows in blocks:
            mean += jnp.sum(ref[rows, :].astype(F32).reshape(block // 8, 8, slots), axis=0)
        mean = jnp.sum(mean, axis=0, keepdims=True) * (1.0 / members)
        info = ref[members:, :].astype(F32)
        prec = info[1:2, :]
        scale = jnp.sqrt(prec)
        weight = prec * (info[0:1, :] - mean)
        for rows in blocks:
            perturb = ref[rows, :].astype(F32) - mean
            near[rows, k * slots : (k + 1) * slots] = (perturb * scale).astype(BF)
            force = jnp.sum(perturb * weight, axis=1, keepdims=True)
            before = force_ref[rows, :] if k == 0 else push[rows, :]
            push[rows, :] = before + jnp.broadcast_to(force, (block, LANES))
    for half in halves:
        wide[:, half] = lax.dot_general(
            near[...], near[half, :], (((1,), (1,)), ((), ())), preferred_element_type=F32
        )
    norm = jnp.zeros((8, members), F32)
    for rows in blocks:
        part = on_diagonal(rows, members - 1.0, wide[rows, :] + sys_ref[rows, :])
        base[rows, :] = part
        base_b[rows, :] = part.astype(BF)
        norm += jnp.sum((part * part).reshape(block // 8, 8, members), axis=0)
    inv = lax.rsqrt(jnp.sum(norm))
    product(base_b, base_b, wide)
    inv2 = inv * inv
    for rows in blocks:
        part = base[rows, :] * inv
        square = wide[rows, :] * inv2
        square_b[rows, :] = square.astype(BF)
        tail_b[rows, :] = (0.0625 * square - 0.5625 * part).astype(BF)
        root[rows, :] = on_diagonal(rows, 2.25, 1.6875 * square - 2.4375 * part)
    product(square_b, tail_b, wide)
    first = jnp.zeros((8, members), F32)
    for rows in blocks:
        part = root[rows, :] + wide[rows, :]
        root[rows, :] = part
        first += jnp.sum((part * push[rows, 0:1]).reshape(block // 8, 8, members), axis=0)
    first = jnp.sum(first, axis=0, keepdims=True) * inv
    means = []
    for start in range(0, members, LANES):
        total = jnp.zeros((8, LANES), F32)
        for rows in (slice(start, start + block), slice(start + block, start + LANES)):
            second = jnp.sum(root[rows, :] * first, axis=1, keepdims=True)
            line = lax.broadcasted_iota(jnp.int32, (block, LANES), 0) + (rows.start - start)
            same = line == lax.broadcasted_iota(jnp.int32, (block, LANES), 1)
            total += jnp.sum(jnp.where(same, second, 0.0).reshape(block // 8, 8, LANES), axis=0)
        means.append(jnp.sum(total, axis=0, keepdims=True))
    mean_row = jnp.concatenate(means, axis=1)
    gain = jnp.sqrt((members - 1.0) * inv)
    for rows in blocks:
        base_b[rows, :] = (gain * root[rows, :] + mean_row).astype(BF)
    for pair in range(tile // 2):
        cols = slice(2 * pair * LANES, 2 * (pair + 1) * LANES)
        new = xbar_ref[0:1, cols] + jnp.dot(
            base_b[...], xb_ref[:, cols], preferred_element_type=F32
        )
        for half in range(2):
            part = new[:, half * LANES : (half + 1) * LANES].astype(BF)
            o_ref[:, 2 * pair + half] = part.reshape(groups, per, LANES)


def place_body(r_ref, o_ref, out, sems):
    lines, members, _ = r_ref.shape
    copies = []
    for q in range(lines // 8):
        flat = out.at[q].reshape(members * 8, LANES)
        for row in range(8):
            flat[pl.ds(row, members, stride=8), :] = r_ref[8 * q + row].astype(F32)
        copy = pltpu.make_async_copy(out.at[q], o_ref.at[:, q], sems.at[q])
        copy.start()
        copies.append(copy)
    for copy in copies:
        copy.wait()


def program(members, diffusivity, advection, obs_value, obs_rinv, obs_cell, obs_count, loc_index):
    per, lines, _ = members.shape
    groups = lax.axis_size("mem")
    regions = lax.axis_size("reg")
    tile = lines // groups
    total = per * groups
    slots = obs_cell.shape[-1]
    near = [(i, i ^ 1) for i in range(regions)]
    across = [(i, (i + 1) % regions if i % 2 else (i - 1) % regions) for i in range(regions)]

    reach = STEPS * per + 16
    send_a, send_b, members, diffusivity, advection = call(
        pack_body,
        [((reach, LANES), BF)] * 2
        + [(v.shape, v.dtype) for v in (members, diffusivity, advection)],
        3,
        [
            pltpu.VMEM((per, 8, LANES), BF),
            pltpu.VMEM((per, 8, LANES), BF),
            pltpu.VMEM((per * 8, LANES), F32),
            pltpu.VMEM((16, LANES), F32),
            pltpu.SemaphoreType.DMA((5,)),
        ],
        specs=[HBM, HBM, HBM],
        moved=1 << 20,
    )(
        *[
            pltpu.with_memory_space_constraint(v, pltpu.HBM)
            for v in (members, diffusivity, advection)
        ]
    )
    got_b = lax.ppermute(send_b, "reg", across)
    got_a = lax.ppermute(send_a, "reg", near)
    picks, info, prec = call(
        prepare_body,
        [((tile * LANES, slots), BF), ((16, slots), BF), ((8, slots), F32)],
        5,
        specs=[VMEM, VMEM, VMEM, SMEM, VMEM],
        moved=1 << 20,
    )(obs_cell, obs_value, obs_rinv, obs_count, loc_index)
    inner, kept = call(
        interior_body,
        [((lines, per, LANES), BF), ((2 * len(KEEP), per, LANES), F32)],
        3,
        [
            pltpu.VMEM((2, lines // 8, BLOCK * 8, LANES), F32),
            pltpu.VMEM((2, lines // 8, BLOCK * 8, LANES), F32),
            pltpu.VMEM((lines, 32, LANES), F32),
        ],
        moved=12 << 20,
    )(members, diffusivity, advection)
    ahead = pl.pallas_call(
        edge_body,
        out_shape=jax.ShapeDtypeStruct((lines, per, LANES), BF),
        in_specs=[pl.BlockSpec(memory_space=pl.ANY)] * 4 + [VMEM] * 5,
        out_specs=pl.BlockSpec(memory_space=pl.ANY),
        input_output_aliases={0: 0},
        scratch_shapes=[
            pltpu.VMEM((2 * STEPS * per, LANES), BF),
            pltpu.VMEM((lines + 8, LANES), F32),
            pltpu.VMEM((lines + 8, LANES), F32),
            pltpu.VMEM((2 * STEPS, per, LANES), BF),
            pltpu.SemaphoreType.DMA((2,)),
        ],
        cost_estimate=pl.CostEstimate(flops=0, bytes_accessed=2 << 20, transcendentals=0),
        compiler_params=pltpu.CompilerParams(vmem_limit_bytes=40 << 20),
        name="edge",
    )(inner, picks, info, prec, kept, got_a, got_b, diffusivity, advection)
    states = lax.all_to_all(ahead.reshape(groups, tile, per, LANES), "mem", 0, 0)
    (obs,) = call(
        observe_body,
        [((total + 16, slots), BF)],
        3,
        flops=2 * total * tile * LANES * slots,
        moved=2 << 20,
    )(states, picks, info)
    nb = lax.ppermute(obs, "reg", across)
    na = lax.ppermute(obs, "reg", near)
    xb, xbar, system, force = call(
        own_body,
        [
            ((total, tile * LANES), BF),
            ((8, tile * LANES), F32),
            ((total, total), F32),
            ((total, LANES), F32),
        ],
        3,
        flops=2 * total * total * slots,
        moved=4 << 20,
    )(states, obs, prec)
    (back,) = call(
        analyse_body,
        [((groups, tile, per, LANES), BF)],
        6,
        [
            pltpu.VMEM((total, 2 * slots), BF),
            pltpu.VMEM((total, total), F32),
            pltpu.VMEM((total, total), BF),
            pltpu.VMEM((total, total), F32),
            pltpu.VMEM((total, total), BF),
            pltpu.VMEM((total, total), BF),
            pltpu.VMEM((total, total), F32),
            pltpu.VMEM((total, LANES), F32),
        ],
        flops=10 * total * total * total,
        moved=4 << 20,
    )(na, nb, xb, xbar, system, force)
    home = lax.all_to_all(back, "mem", 0, 0).reshape(lines, per, LANES)
    placed = pl.pallas_call(
        place_body,
        out_shape=jax.ShapeDtypeStruct((per, lines // 8, 8, LANES), F32),
        in_specs=[VMEM],
        out_specs=HBM,
        scratch_shapes=[
            pltpu.VMEM((lines // 8, per, 8, LANES), F32),
            pltpu.SemaphoreType.DMA((lines // 8,)),
        ],
        compiler_params=pltpu.CompilerParams(vmem_limit_bytes=40 << 20),
        name="place",
    )(home)
    return placed.reshape(per, lines, LANES)


def solution(mesh):
    return jax.shard_map(
        program,
        mesh=mesh,
        in_specs=(
            P("mem", "reg", None),
            P("reg", None),
            P("reg", None),
            P("reg", "mem", None),
            P("reg", "mem", None),
            P("reg", "mem", None),
            P("reg", "mem"),
            P("reg", "mem", None),
        ),
        out_specs=P("mem", "reg", None),
        check_vma=False,
    )
```

```python
import jax
import jax.numpy as jnp
from jax import lax
from jax.experimental import pallas as pl
from jax.experimental.pallas import tpu as pltpu
from jax.sharding import PartitionSpec as P

STEPS = 3
LANES = 128
BLOCK = 32
BF = jnp.bfloat16
F32 = jnp.float32
VMEM = pl.BlockSpec(memory_space=pltpu.VMEM)
SMEM = pl.BlockSpec(memory_space=pltpu.SMEM)
HBM = pl.BlockSpec(memory_space=pltpu.HBM)


def call(body, outs, n_in, scratch=(), specs=None, flops=0, moved=0, grant=40 << 20):
    return pl.pallas_call(
        body,
        out_shape=[jax.ShapeDtypeStruct(s, d) for s, d in outs],
        in_specs=specs or [VMEM] * n_in,
        out_specs=[VMEM] * len(outs),
        scratch_shapes=list(scratch),
        cost_estimate=pl.CostEstimate(flops=flops, bytes_accessed=moved, transcendentals=0),
        compiler_params=pltpu.CompilerParams(vmem_limit_bytes=grant),
    )


def pack_body(x_ref, d_ref, a_ref, sa_ref, sb_ref, xv_ref, dv_ref, av_ref, rows, coef, sems):
    members = x_ref.shape[0]
    lines = x_ref.shape[1]
    count = lines // 8

    def rows_of(q):
        here = pl.ds(8 * q, 8)
        return pltpu.make_async_copy(x_ref.at[:, here, :], xv_ref.at[:, here, :], sems.at[q])

    edges = [rows_of(0), rows_of(count - 1)] + [
        pltpu.make_async_copy(d_ref, dv_ref, sems.at[count]),
        pltpu.make_async_copy(a_ref, av_ref, sems.at[count + 1]),
    ]
    inner = [rows_of(q) for q in range(1, count - 1)]
    for copy in edges + inner:
        copy.start()
    for copy in edges:
        copy.wait()

    def edge(out_ref, side):
        base = (lines - 8) * side
        rows[...] = xv_ref[:, base : base + 8, :].astype(F32).reshape(members * 8, LANES)
        first = (8 - STEPS) * side
        for k in range(STEPS):
            out_ref[k * members : (k + 1) * members, :] = rows[
                pl.ds(first + k, members, stride=8), :
            ].astype(BF)
        at = (lines - 2) * side
        coef[0:2, :] = dv_ref[at : at + 2, :]
        coef[2:4, :] = av_ref[at : at + 2, :]
        whole = coef[0:4, :]
        high = whole.astype(BF).astype(F32)
        middle = (whole - high).astype(BF).astype(F32)
        coef[0:4, :] = high
        coef[4:8, :] = middle
        coef[8:12, :] = whole - high - middle
        coef[12:16, :] = jnp.zeros((4, LANES), F32)
        out_ref[STEPS * members :, :] = coef[...].astype(BF)

    even = lax.rem(lax.axis_index("reg"), 2) == 0

    @pl.when(even)
    def _():
        edge(sa_ref, 1)
        edge(sb_ref, 0)

    @pl.when(jnp.logical_not(even))
    def _():
        edge(sa_ref, 0)
        edge(sb_ref, 1)

    for copy in inner:
        copy.wait()


def laplace():
    i = lax.broadcasted_iota(jnp.int32, (LANES, LANES), 0)
    j = lax.broadcasted_iota(jnp.int32, (LANES, LANES), 1)
    gap = jnp.bitwise_and(i - j, LANES - 1)
    beside = jnp.logical_or(gap == 1, gap == LANES - 1)
    return jnp.where(gap == 0, -4.0, jnp.where(beside, 1.0, 0.0)).astype(BF)


def beside():
    i = lax.broadcasted_iota(jnp.int32, (LANES, LANES), 0)
    j = lax.broadcasted_iota(jnp.int32, (LANES, LANES), 1)
    gap = jnp.bitwise_and(i - j, LANES - 1)
    once = jnp.where(jnp.logical_or(gap == 1, gap == LANES - 1), 1.0, 0.0).astype(BF)
    return jnp.concatenate([once, once], axis=0)


def rolled(centre):
    return pltpu.roll(centre, 1, 1) + pltpu.roll(centre, LANES - 1, 1)


def sides_of(centre, pair):
    high = centre.astype(BF)
    low = (centre - high.astype(F32)).astype(BF)
    both = jnp.concatenate([high, low], axis=1)
    return jnp.dot(both, pair, preferred_element_type=F32)


KEEP = ((0, 0), (0, 1), ("lap", 0), (1, 1), (1, 2), (2, 2), (2, 3))


def interior_body(x_ref, d_ref, a_ref, o_ref, k_ref, xs, ls, cf):
    members = x_ref.shape[0]
    lines = x_ref.shape[1]
    for row in range(lines):
        dif = jnp.broadcast_to(d_ref[row : row + 1, :], (8, LANES))
        adv = 0.5 * jnp.broadcast_to(a_ref[row : row + 1, :], (8, LANES))
        cf[row, 0:8, :] = 1.0 - 4.0 * dif
        cf[row, 8:16, :] = dif
        cf[row, 16:24, :] = dif + adv
        cf[row, 24:32, :] = dif - adv
    across = laplace()
    pair = beside()
    block = BLOCK

    def stage(b, slot):
        here = pl.ds(b * block, block)
        for q in range(lines // 8):
            part = x_ref[here, 8 * q : 8 * q + 8, :].astype(F32).reshape(block * 8, LANES)
            xs[slot, q] = part
            ls[slot, q] = jnp.dot(part.astype(BF), across, preferred_element_type=F32)

    def c(row, k):
        v = cf[row, 8 * k : 8 * k + 8, :]
        return jnp.concatenate([v] * (block // 8), axis=0)

    def advance(b, slot):
        here = pl.ds(b * block, block)

        def keep(what, row, value):
            for side in range(2):
                away = lines - 1 - row if side else row
                if (what, away) in KEEP:
                    k_ref[side * len(KEEP) + KEEP.index((what, away)), here, :] = value

        levels = [{} for _ in range(STEPS + 1)]
        for row in range(lines):
            at_row = pl.ds(row % 8, block, stride=8)
            levels[0][row] = xs[slot, row // 8, at_row, :]
            keep(0, row, levels[0][row])
            if row in (0, lines - 1):
                keep("lap", row, ls[slot, row // 8, at_row, :])
            for level in range(1, STEPS + 1):
                at = row - level
                if at < level or at + level >= lines:
                    continue
                prev = levels[level - 1]
                centre = prev[at]
                vertical = c(at, 2) * prev[at - 1] + c(at, 3) * prev[at + 1]
                if level == 1:
                    lap = ls[slot, at // 8, pl.ds(at % 8, block, stride=8), :]
                    new = centre + c(at, 1) * lap + vertical
                else:
                    new = c(at, 0) * centre + c(at, 1) * (sides_of(centre, pair) if level == 2 else rolled(centre)) + vertical
                keep(level, at, new)
                if level == STEPS:
                    o_ref[at, here, :] = new.astype(BF)
                else:
                    levels[level][at] = new
                del prev[at - 1]

    count = members // block
    stage(0, 0)
    for b in range(count):
        if b + 1 < count:
            stage(b + 1, (b + 1) % 2)
        advance(b, b % 2)


def edge_body(f_ref, picks_ref, info_ref, prec_ref, k_ref, ra_ref, rb_ref, d_ref, a_ref, *rest):
    del f_ref, picks_ref, info_ref, prec_ref
    o_ref, halo, dd, aa, new_rows, sems = rest
    members = k_ref.shape[1]
    lines = d_ref.shape[0]
    reach = STEPS * members
    even = lax.rem(lax.axis_index("reg"), 2) == 0

    def take(ref, side):
        halo[side * reach : (side + 1) * reach, :] = ref[0:reach, :]
        parts = ref[reach:, :].astype(F32)
        whole = parts[0:4] + parts[4:8] + parts[8:12]
        at = (lines + 2) if side else 0
        dd[at : at + 2, :] = whole[0:2]
        aa[at : at + 2, :] = whole[2:4]

    @pl.when(even)
    def _():
        take(rb_ref, 0)
        take(ra_ref, 1)

    @pl.when(jnp.logical_not(even))
    def _():
        take(ra_ref, 0)
        take(rb_ref, 1)

    dd[2 : 2 + lines, :] = d_ref[...]
    aa[2 : 2 + lines, :] = a_ref[...]
    across = laplace()
    pair = beside()
    copies = []
    for side in range(2):

        def at(away):
            return lines - 1 - away if side else away

        def coefs(away):
            row = at(away) + 2
            dif = jnp.broadcast_to(dd[row : row + 1, :], (members, LANES))
            adv = 0.5 * jnp.broadcast_to(aa[row : row + 1, :], (members, LANES))
            inward = dif - adv if side == 0 else dif + adv
            outward = dif + adv if side == 0 else dif - adv
            return dif, outward, inward

        def outer(away):
            k = (-away - 1) if side else (STEPS + away)
            start = side * reach + k * members
            return halo[start : start + members, :]

        def kept(what, away):
            return k_ref[side * len(KEEP) + KEEP.index((what, away))]

        states = [{} for _ in range(STEPS)]
        for away in range(-STEPS, 0):
            states[0][away] = outer(away).astype(F32)
        for what, away in KEEP:
            if what != "lap":
                states[what][away] = kept(what, away)
        for level in range(1, STEPS + 1):
            prev = states[level - 1]
            for away in range(level - STEPS, level):
                dif, outward, inward = coefs(away)
                vertical = outward * prev[away - 1] + inward * prev[away + 1]
                centre = prev[away]
                if level == 1:
                    lap = (
                        kept("lap", 0)
                        if away == 0
                        else jnp.dot(outer(away), across, preferred_element_type=F32)
                    )
                    new = centre + dif * lap + vertical
                else:
                    around = jnp.dot(
                        centre.astype(BF), pair[:LANES], preferred_element_type=F32
                    )
                    new = (1.0 - 4.0 * dif) * centre + dif * around + vertical
                if level == STEPS:
                    slot = STEPS - 1 - away if side else away
                    new_rows[side * STEPS + slot] = new.astype(BF)
                else:
                    states[level][away] = new
        first = lines - STEPS if side else 0
        copy = pltpu.make_async_copy(
            new_rows.at[pl.ds(side * STEPS, STEPS)],
            o_ref.at[pl.ds(first, STEPS)],
            sems.at[side],
        )
        copy.start()
        copies.append(copy)
    for copy in copies:
        copy.wait()


def prepare_body(cell_ref, value_ref, rinv_ref, count_ref, loc_ref, picks_ref, info_ref, prec_ref):
    cells, slots = picks_ref.shape
    cell = cell_ref[0]
    line = lax.broadcasted_iota(jnp.int32, (cells, slots), 0)
    picks_ref[...] = jnp.where(line == cell, 1.0, 0.0).astype(BF)
    slot = lax.broadcasted_iota(jnp.int32, (1, slots), 1)
    own = jnp.where(slot < count_ref[0, 0], rinv_ref[0], 0.0)
    radius = (loc_ref[0].astype(F32) + 1.0) / 4.0
    far = own * jnp.exp(-(radius * radius))
    row = lax.broadcasted_iota(jnp.int32, (16, slots), 0)
    value = value_ref[0].astype(F32)
    info_ref[...] = jnp.where(row == 0, value, jnp.where(row == 1, far, 0.0)).astype(BF)
    prec_ref[...] = jnp.where(
        lax.broadcasted_iota(jnp.int32, (8, slots), 0) == 0, own, value
    )


def observe_body(s_ref, picks_ref, info_ref, h_ref):
    groups, tile, per, _ = s_ref.shape
    members = groups * per
    total = jnp.zeros((members, picks_ref.shape[1]), F32)
    for pair in range(tile // 2):
        here = jnp.concatenate(
            [
                s_ref[:, 2 * pair].reshape(members, LANES),
                s_ref[:, 2 * pair + 1].reshape(members, LANES),
            ],
            axis=1,
        )
        picks = picks_ref[2 * LANES * pair : 2 * LANES * (pair + 1), :]
        total += jnp.dot(here, picks, preferred_element_type=F32)
    h_ref[0:members, :] = total.astype(BF)
    h_ref[members:, :] = info_ref[...]


def weigh(obs, value, prec):
    count = obs.shape[0]
    mean = jnp.sum(obs, axis=0, keepdims=True) * (1.0 / count)
    perturb = obs - mean
    scaled = (perturb * jnp.sqrt(prec)).astype(BF)
    force = jnp.sum(perturb * (prec * (value - mean)), axis=1, keepdims=True)
    return scaled, force


def gram(a):
    return lax.dot_general(a, a, (((1,), (1,)), ((), ())), preferred_element_type=F32)


def own_body(s_ref, h_ref, prec_ref, xb_ref, xbar_ref, sys_ref, force_ref):
    groups, tile, per, _ = s_ref.shape
    members = groups * per
    for row in range(tile):
        here = s_ref[:, row].reshape(members, LANES).astype(F32)
        mean = jnp.sum(here, axis=0, keepdims=True) * (1.0 / members)
        xbar_ref[:, row * LANES : (row + 1) * LANES] = jnp.broadcast_to(mean, (8, LANES))
        xb_ref[:, row * LANES : (row + 1) * LANES] = (here - mean).astype(BF)
    scaled, force = weigh(h_ref[0:members, :].astype(F32), prec_ref[1:2, :], prec_ref[0:1, :])
    sys_ref[...] = gram(scaled)
    force_ref[...] = jnp.broadcast_to(force, (members, LANES))


def weigh_into(ref, near, first_col, force_ref, push):
    members = near.shape[0]
    slots = ref.shape[1]
    block = 64
    blocks = [slice(i, i + block) for i in range(0, members, block)]
    mean = jnp.zeros((8, slots), F32)
    for rows in blocks:
        mean += jnp.sum(ref[rows, :].astype(F32).reshape(block // 8, 8, slots), axis=0)
    mean = jnp.sum(mean, axis=0, keepdims=True) * (1.0 / members)
    info = ref[members:, :].astype(F32)
    prec = info[1:2, :]
    scale = jnp.sqrt(prec)
    weight = prec * (info[0:1, :] - mean)
    for rows in blocks:
        perturb = ref[rows, :].astype(F32) - mean
        near[rows, first_col : first_col + slots] = (perturb * scale).astype(BF)
        force = jnp.sum(perturb * weight, axis=1, keepdims=True)
        push[rows, :] = force_ref[rows, :] + jnp.broadcast_to(force, (block, LANES))


def near_body(r_ref, sys_ref, force_ref, out_ref, push_ref, near):
    members = sys_ref.shape[0]
    weigh_into(r_ref, near, 0, force_ref, push_ref)
    for start in range(0, members, 2 * LANES):
        half = slice(start, start + 2 * LANES)
        out_ref[:, half] = sys_ref[:, half] + lax.dot_general(
            near[...], near[half, :], (((1,), (1,)), ((), ())), preferred_element_type=F32
        )


def analyse_body(r_ref, xb_ref, xbar_ref, sys_ref, force_ref, o_ref, *scratch):
    near, base, base_b, wide, square_b, tail_b, root, push = scratch
    members = sys_ref.shape[0]
    groups, tile, per, _ = o_ref.shape
    block = 64
    blocks = [slice(i, i + block) for i in range(0, members, block)]
    halves = [slice(i, i + 2 * LANES) for i in range(0, members, 2 * LANES)]

    def on_diagonal(rows, value, other):
        first = rows.start // LANES * LANES
        line = lax.broadcasted_iota(jnp.int32, (block, LANES), 0) + (rows.start - first)
        same = line == lax.broadcasted_iota(jnp.int32, (block, LANES), 1)
        mine = other[:, first : first + LANES] + jnp.where(same, value, 0.0)
        parts = [other[:, :first], mine, other[:, first + LANES :]]
        return jnp.concatenate([p for p in parts if p.shape[1]], axis=1)

    def product(left, right, into):
        for half in halves:
            into[:, half] = jnp.dot(left[...], right[:, half], preferred_element_type=F32)

    weigh_into(r_ref, near, 0, force_ref, push)
    for half in halves:
        wide[:, half] = lax.dot_general(
            near[...], near[half, :], (((1,), (1,)), ((), ())), preferred_element_type=F32
        )
    norm = jnp.zeros((8, members), F32)
    for rows in blocks:
        part = on_diagonal(rows, members - 1.0, wide[rows, :] + sys_ref[rows, :])
        base[rows, :] = part
        base_b[rows, :] = part.astype(BF)
        norm += jnp.sum((part * part).reshape(block // 8, 8, members), axis=0)
    inv = lax.rsqrt(jnp.sum(norm))
    product(base_b, base_b, wide)
    inv2 = inv * inv
    for rows in blocks:
        part = base[rows, :] * inv
        square = wide[rows, :] * inv2
        square_b[rows, :] = square.astype(BF)
        tail_b[rows, :] = (0.0625 * square - 0.5625 * part).astype(BF)
        root[rows, :] = on_diagonal(rows, 2.25, 1.6875 * square - 2.4375 * part)
    product(square_b, tail_b, wide)
    first = jnp.zeros((8, members), F32)
    for rows in blocks:
        part = root[rows, :] + wide[rows, :]
        root[rows, :] = part
        first += jnp.sum((part * push[rows, 0:1]).reshape(block // 8, 8, members), axis=0)
    first = jnp.sum(first, axis=0, keepdims=True) * inv
    means = []
    for start in range(0, members, LANES):
        total = jnp.zeros((8, LANES), F32)
        for rows in (slice(start, start + block), slice(start + block, start + LANES)):
            second = jnp.sum(root[rows, :] * first, axis=1, keepdims=True)
            line = lax.broadcasted_iota(jnp.int32, (block, LANES), 0) + (rows.start - start)
            same = line == lax.broadcasted_iota(jnp.int32, (block, LANES), 1)
            total += jnp.sum(jnp.where(same, second, 0.0).reshape(block // 8, 8, LANES), axis=0)
        means.append(jnp.sum(total, axis=0, keepdims=True))
    mean_row = jnp.concatenate(means, axis=1)
    gain = jnp.sqrt((members - 1.0) * inv)
    for rows in blocks:
        base_b[rows, :] = (gain * root[rows, :] + mean_row).astype(BF)
    for pair in range(tile // 2):
        cols = slice(2 * pair * LANES, 2 * (pair + 1) * LANES)
        new = xbar_ref[0:1, cols] + jnp.dot(
            base_b[...], xb_ref[:, cols], preferred_element_type=F32
        )
        for half in range(2):
            part = new[:, half * LANES : (half + 1) * LANES].astype(BF)
            o_ref[:, 2 * pair + half] = part.reshape(groups, per, LANES)


def place_body(r_ref, o_ref, out, sems):
    lines, members, _ = r_ref.shape
    copies = []
    for q in range(lines // 8):
        flat = out.at[q].reshape(members * 8, LANES)
        for row in range(8):
            flat[pl.ds(row, members, stride=8), :] = r_ref[8 * q + row].astype(F32)
        copy = pltpu.make_async_copy(out.at[q], o_ref.at[:, q], sems.at[q])
        copy.start()
        copies.append(copy)
    for copy in copies:
        copy.wait()


def program(members, diffusivity, advection, obs_value, obs_rinv, obs_cell, obs_count, loc_index):
    per, lines, _ = members.shape
    groups = lax.axis_size("mem")
    regions = lax.axis_size("reg")
    tile = lines // groups
    total = per * groups
    slots = obs_cell.shape[-1]
    near = [(i, i ^ 1) for i in range(regions)]
    across = [(i, (i + 1) % regions if i % 2 else (i - 1) % regions) for i in range(regions)]

    reach = STEPS * per + 16
    send_a, send_b, members, diffusivity, advection = call(
        pack_body,
        [((reach, LANES), BF)] * 2
        + [(v.shape, v.dtype) for v in (members, diffusivity, advection)],
        3,
        [
            pltpu.VMEM((per * 8, LANES), F32),
            pltpu.VMEM((16, LANES), F32),
            pltpu.SemaphoreType.DMA((lines // 8 + 2,)),
        ],
        specs=[HBM, HBM, HBM],
        moved=1 << 20,
    )(
        *[
            pltpu.with_memory_space_constraint(v, pltpu.HBM)
            for v in (members, diffusivity, advection)
        ]
    )
    got_b = lax.ppermute(send_b, "reg", across)
    got_a = lax.ppermute(send_a, "reg", near)
    picks, info, prec = call(
        prepare_body,
        [((tile * LANES, slots), BF), ((16, slots), BF), ((8, slots), F32)],
        5,
        specs=[VMEM, VMEM, VMEM, SMEM, VMEM],
        moved=1 << 20,
    )(obs_cell, obs_value, obs_rinv, obs_count, loc_index)
    inner, kept = call(
        interior_body,
        [((lines, per, LANES), BF), ((2 * len(KEEP), per, LANES), F32)],
        3,
        [
            pltpu.VMEM((2, lines // 8, BLOCK * 8, LANES), F32),
            pltpu.VMEM((2, lines // 8, BLOCK * 8, LANES), F32),
            pltpu.VMEM((lines, 32, LANES), F32),
        ],
        moved=12 << 20,
    )(members, diffusivity, advection)
    ahead = pl.pallas_call(
        edge_body,
        out_shape=jax.ShapeDtypeStruct((lines, per, LANES), BF),
        in_specs=[pl.BlockSpec(memory_space=pl.ANY)] * 4 + [VMEM] * 5,
        out_specs=pl.BlockSpec(memory_space=pl.ANY),
        input_output_aliases={0: 0},
        scratch_shapes=[
            pltpu.VMEM((2 * STEPS * per, LANES), BF),
            pltpu.VMEM((lines + 8, LANES), F32),
            pltpu.VMEM((lines + 8, LANES), F32),
            pltpu.VMEM((2 * STEPS, per, LANES), BF),
            pltpu.SemaphoreType.DMA((2,)),
        ],
        cost_estimate=pl.CostEstimate(flops=0, bytes_accessed=2 << 20, transcendentals=0),
        compiler_params=pltpu.CompilerParams(vmem_limit_bytes=40 << 20),
        name="edge",
    )(inner, picks, info, prec, kept, got_a, got_b, diffusivity, advection)
    states = lax.all_to_all(ahead.reshape(groups, tile, per, LANES), "mem", 0, 0)
    (obs,) = call(
        observe_body,
        [((total + 16, slots), BF)],
        3,
        flops=2 * total * tile * LANES * slots,
        moved=2 << 20,
    )(states, picks, info)
    nb = lax.ppermute(obs, "reg", across)
    na = lax.ppermute(obs, "reg", near)
    xb, xbar, system, force = call(
        own_body,
        [
            ((total, tile * LANES), BF),
            ((8, tile * LANES), F32),
            ((total, total), F32),
            ((total, LANES), F32),
        ],
        3,
        flops=2 * total * total * slots,
        moved=4 << 20,
    )(states, obs, prec)
    system, force = call(
        near_body,
        [((total, total), F32), ((total, LANES), F32)],
        3,
        [pltpu.VMEM((total, slots), BF)],
        flops=2 * total * total * slots,
        moved=4 << 20,
    )(na, system, force)
    (back,) = call(
        analyse_body,
        [((groups, tile, per, LANES), BF)],
        5,
        [
            pltpu.VMEM((total, slots), BF),
            pltpu.VMEM((total, total), F32),
            pltpu.VMEM((total, total), BF),
            pltpu.VMEM((total, total), F32),
            pltpu.VMEM((total, total), BF),
            pltpu.VMEM((total, total), BF),
            pltpu.VMEM((total, total), F32),
            pltpu.VMEM((total, LANES), F32),
        ],
        flops=10 * total * total * total,
        moved=4 << 20,
    )(nb, xb, xbar, system, force)
    home = lax.all_to_all(back, "mem", 0, 0).reshape(lines, per, LANES)
    placed = pl.pallas_call(
        place_body,
        out_shape=jax.ShapeDtypeStruct((per, lines // 8, 8, LANES), F32),
        in_specs=[VMEM],
        out_specs=HBM,
        scratch_shapes=[
            pltpu.VMEM((lines // 8, per, 8, LANES), F32),
            pltpu.SemaphoreType.DMA((lines // 8,)),
        ],
        compiler_params=pltpu.CompilerParams(vmem_limit_bytes=40 << 20),
        name="place",
    )(home)
    return placed.reshape(per, lines, LANES)


def solution(mesh):
    return jax.shard_map(
        program,
        mesh=mesh,
        in_specs=(
            P("mem", "reg", None),
            P("reg", None),
            P("reg", None),
            P("reg", "mem", None),
            P("reg", "mem", None),
            P("reg", "mem", None),
            P("reg", "mem"),
            P("reg", "mem", None),
        ),
        out_specs=P("mem", "reg", None),
        check_vma=False,
    )
```
